32 devices in a mesh: fsdp: 8 (over y, x, core), blk: 4 (over z).
Axes of the slice: x: 2, y: 2, z: 4, core: 2. Of those that a mesh axis runs over, the one named last changes fastest.
Arguments:
- grad: bfloat16 [16, 768, 768], P(None, 'fsdp', 'blk'), may hold values from -16 to 16
- owner_slots: int32 [16], replicated, may hold values from 0 to 15, as said below
- stat_left: float32 [16, 768, 768], P('fsdp', None, 'blk'), may hold values from -6 to 6
- stat_right: float32 [16, 768, 768], P('fsdp', None, 'blk'), may hold values from -6 to 6
- basis_left: bfloat16 [16, 768, 768], P('fsdp'), may hold values from -1 to 1, as said below
- basis_right: bfloat16 [16, 768, 768], P('fsdp'), may hold values from -1 to 1, as said below
- moment: float32 [16, 768, 768], P('fsdp', None, 'blk'), may hold values from -3 to 3
- second: float32 [16, 768, 768], P('fsdp', None, 'blk'), may hold values from 0.01 to 0.1
Outputs:
- update: bfloat16 [16, 768, 768], P(None, 'fsdp', 'blk')
- new_left: float32 [16, 768, 768], P('fsdp', None, 'blk')
- new_right: float32 [16, 768, 768], P('fsdp', None, 'blk')
- new_moment: float32 [16, 768, 768], P('fsdp', None, 'blk')
- new_second: float32 [16, 768, 768], P('fsdp', None, 'blk')
- grad_rms: float32 [], replicated
The draws below stay inside these ranges and needn't reach their ends.
Inputs may be any that keep to these rules, and one draw needn't show every extreme that they name: Each 768 x 768 block of basis_left is orthogonal up to bfloat16 rounding. Each 768 x 768 block of basis_right is orthogonal up to bfloat16 rounding. owner_slots names every block exactly once.
All inputs are finite; a program needn't handle non-finite values.
Results may differ from the reference program's by a relative error of at most 0.0058.
Values may be sent and summed in bfloat16 or wider, within the bound.
No kernel may reach another device: no remote copies, remote signals or barrier semaphores. Data moves between devices by JAX's collectives and lax.ppermute only.
A program may use at most 64 MiB of HBM per device.

```python
import math
import jax
import jax.numpy as jnp
from jax import lax

BS = 768
NBG = 16


def slot_order(key):
    return jax.random.permutation(jax.random.fold_in(key, 77), NBG).astype(jnp.int32)


def draw_owner_slots(key, part):
    return slot_order(key)


def draw_grad(key, part):
    slots = slot_order(key)
    places = jnp.zeros((NBG,), jnp.int32).at[slots].set(jnp.arange(NBG, dtype=jnp.int32))
    level = places.astype(jnp.float32) / (NBG - 1)
    inner = jax.random.fold_in(key, 5)
    rows = jnp.arange(BS, dtype=jnp.float32)
    row_scale = jnp.sqrt(1.0 + 2.0 * rows / (BS - 1))
    scale = row_scale[None, :, None] * row_scale[None, None, :]
    block_scale = jnp.sqrt(1.0 + 8.0 * level)
    values = 0.5 * jax.random.normal(inner, (NBG, BS, BS), jnp.float32) * scale * block_scale[:, None, None]
    return jnp.clip(values, -16.0, 16.0).astype(jnp.bfloat16)


def orthogonal(key):
    matrix = jax.random.normal(key, (NBG, BS, BS), jnp.float32)
    basis, upper = jnp.linalg.qr(matrix)
    return basis.astype(jnp.bfloat16)


def draw_basis_left(key, part):
    return orthogonal(jax.random.fold_in(key, 11))


def draw_basis_right(key, part):
    return orthogonal(jax.random.fold_in(key, 23))


def block_levels(own_key, shape, split, low, top_value):
    level = 1.0
    for position, parts in split:
        draws = jax.random.uniform(jax.random.fold_in(jax.random.fold_in(own_key, 6), position), (parts,), jnp.float32, low / len(split), top_value / len(split))
        level = level * jnp.repeat(jnp.exp(draws), shape[position] // parts).reshape((-1,) + (1,) * (len(shape) - 1 - position))
    return level


def centred(stream_key, dims, scale, reach, cuts=(), kind=jnp.bfloat16):
    drawn = jax.random.normal(stream_key, dims, jnp.float32) * scale
    if len(cuts) > 0:
        drawn = block_levels(stream_key, dims, cuts, -0.22, 0.18) * drawn
    return jnp.clip(drawn, min=-reach, max=reach).astype(kind)


def setup_inputs(seed: int = 0) -> dict:
    seeds = jax.random.split(jax.random.key(seed), 9)
    return {
        "grad": draw_grad(jax.random.fold_in(seeds[8], 71), 0),
        "owner_slots": draw_owner_slots(jax.random.fold_in(seeds[8], 71), 0),
        "stat_left": centred(seeds[2], (NBG, BS, BS), 1.0, 6.0, ((0, 8), (2, 4)), jnp.float32),
        "stat_right": centred(seeds[3], (NBG, BS, BS), 1.0, 6.0, ((0, 8), (2, 4)), jnp.float32),
        "basis_left": draw_basis_left(jax.random.fold_in(seeds[8], 71), 0),
        "basis_right": draw_basis_right(jax.random.fold_in(seeds[8], 71), 0),
        "moment": centred(seeds[6], (NBG, BS, BS), 0.2, 3.0, ((0, 8), (2, 4)), jnp.float32),
        "second": jnp.clip(jnp.exp(math.log(0.1) - 2.3025851 * jax.random.uniform(seeds[7], (NBG, BS, BS), jnp.float32) ** block_levels(seeds[7], (NBG, BS, BS), ((0, 8), (2, 4)), -0.2, 0.2)), 0.01, 0.1),
    }


clip_level = 0.5
stat_decay = 0.95
beta_one = 0.9
beta_two = 0.95
epsilon = 1e-08

def reference(grad, owner_slots, stat_left, stat_right, basis_left, basis_right, moment, second):
    total = jnp.sum(jnp.square(grad.astype(jnp.float32)))
    grad_rms = jnp.sqrt(total / (NBG * BS * BS))
    factor = jnp.minimum(1.0, clip_level / grad_rms)

    def one_block(index):
        which = owner_slots[index]
        block = grad[which]
        q_left = basis_left[index]
        q_right = basis_right[index]
        outer_left = jnp.dot(block.astype(jnp.float32), block.T.astype(jnp.float32), preferred_element_type=jnp.float32)
        outer_right = jnp.dot(block.T.astype(jnp.float32), block.astype(jnp.float32), preferred_element_type=jnp.float32)
        new_l = stat_decay * stat_left[index] + (1.0 - stat_decay) * (factor * factor) * outer_left
        new_r = stat_decay * stat_right[index] + (1.0 - stat_decay) * (factor * factor) * outer_right
        turned = jnp.dot(block.astype(jnp.float32), q_right.astype(jnp.float32), preferred_element_type=jnp.float32).astype(jnp.bfloat16)
        rotated = factor * jnp.dot(q_left.T.astype(jnp.float32), turned.astype(jnp.float32), preferred_element_type=jnp.float32)
        new_m = beta_one * moment[index] + (1.0 - beta_one) * rotated
        new_v = beta_two * second[index] + (1.0 - beta_two) * rotated * rotated
        scaled = (new_m / (jnp.sqrt(new_v) + epsilon)).astype(jnp.bfloat16)
        back = jnp.dot(q_left.astype(jnp.float32), scaled.astype(jnp.float32), preferred_element_type=jnp.float32).astype(jnp.bfloat16)
        step = jnp.dot(back.astype(jnp.float32), q_right.T.astype(jnp.float32), preferred_element_type=jnp.float32).astype(jnp.bfloat16)
        return (step, new_l, new_r, new_m, new_v)
    steps, new_left, new_right, new_moment, new_second = lax.map(one_block, jnp.arange(NBG, dtype=jnp.int32))
    update = jnp.zeros_like(steps).at[owner_slots].set(steps)
    return (update, new_left, new_right, new_moment, new_second, grad_rms)
```

```python
import jax
import jax.numpy as jnp
from jax import lax
from jax.sharding import PartitionSpec as P


clip_level = 0.5
stat_decay = 0.95
beta_one = 0.9
beta_two = 0.95
epsilon = 1e-08


def dot(a, b, da, db):
    return lax.dot_general(a, b, (((da,), (db,)), ((), ())), preferred_element_type=jnp.float32)


def total_over(value, axes):
    for name in axes:
        size = lax.axis_size(name)
        if size & (size - 1):
            value = lax.psum(value, name)
            continue
        step = 1
        while step < size:
            value = value + lax.ppermute(value, name, [(i, i ^ step) for i in range(size)])
            step *= 2
    return value


def after(value, *earlier):
    return lax.optimization_barrier((value,) + earlier)[0]


def send(value, pairs):
    return lax.ppermute(value, "blk", pairs)


SWAP = [(0, 1), (1, 0), (2, 3), (3, 2)]
MIDDLE = [(1, 2), (2, 1)]
OVER = [(0, 2), (3, 1)]
INWARD = [(0, 1), (3, 2)]
OUTWARD = [(1, 0), (2, 3)]


def moments(turned, basis, factor, moment, second):
    rotated = factor * dot(turned, basis, 1, 0)
    new_moment = beta_one * moment + (1.0 - beta_one) * rotated
    new_second = beta_two * second + (1.0 - beta_two) * rotated * rotated
    scaled = (new_moment / (jnp.sqrt(new_second) + epsilon)).astype(jnp.bfloat16)
    back = dot(scaled, basis, 1, 1).astype(jnp.bfloat16)
    return new_moment, new_second, back


def whole_step(grad, owner_slots, stat_left, stat_right, basis_left, basis_right, moment, second):
    blocks, rows, width = grad.shape
    owners = lax.axis_size("fsdp")
    size = lax.axis_size("blk")
    per = blocks // owners
    order = rows * owners
    place = lax.axis_index("blk")
    line = size == 4
    slots = owner_slots.reshape(owners, per)

    own = []
    for s in range(per):
        sent = grad.at[slots[:, s]].get(mode="promise_in_bounds", unique_indices=True)
        piece = lax.all_to_all(sent, "fsdp", split_axis=0, concat_axis=0, tiled=True)
        own.append(piece.reshape(order, width).T)

    partial_sum = jnp.sum(jnp.square(grad.astype(jnp.float32))).reshape(1, 1)
    total = total_over(partial_sum, ("fsdp", "blk"))[0, 0]
    grad_rms = jnp.sqrt(total / (blocks * order * order))
    factor = jnp.minimum(1.0, clip_level / grad_rms)

    upper = place >= 2
    end = (place == 0) | (place == 3)
    if line:
        near_at = jnp.where(upper, 1, 2)
        ids = [place, place ^ 1, near_at, jnp.where(upper, 0, 3)]
    else:
        ids = [lax.rem(place + k, size) for k in range(size)]

    def rearranged(matrix):
        matrix = jnp.concatenate([lax.dynamic_slice_in_dim(matrix, i * width, width, 0) for i in ids], axis=0)
        return jnp.concatenate([lax.dynamic_slice_in_dim(matrix, i * width, width, 1) for i in ids], axis=1)

    turn = []
    for s in range(per):
        turn.append(rearranged(basis_right[s]))

    def canonical(parts):
        if line:
            a, b, c, d = parts
            low = jnp.where(place == 0, a, b), jnp.where(place == 0, b, a)
            high = jnp.where(place == 2, a, b), jnp.where(place == 2, b, a)
            return [
                jnp.where(upper, d, low[0]),
                jnp.where(upper, c, low[1]),
                jnp.where(upper, high[0], c),
                jnp.where(upper, high[1], d),
            ]
        return [sum(jnp.where(i == k, p, 0) for i, p in zip(ids, parts)) for k in range(len(parts))]

    gathered = []
    if line:
        held = None
        for s in range(per):
            pair = send(own[s], SWAP)
            block = own[s] if held is None else after(own[s], *held)
            near = send(block, MIDDLE)
            far = send(block, OVER)
            held = (near, far)
            passed = send(jnp.stack([near, far]), OUTWARD)
            near, far = jnp.where(end, passed[0], near), jnp.where(end, passed[1], far)
            gathered.append([own[s], pair, near, far])
    else:
        for s in range(per):
            every = lax.all_gather(own[s], "blk")
            gathered.append([lax.dynamic_index_in_dim(every, i, 0, keepdims=False) for i in ids])

    lefts, rights, moms, secs = [], [], [], []
    placed = jnp.zeros_like(grad)
    for s in range(per):
        columns = jnp.concatenate(gathered[s], axis=0)
        turned = dot(turn[s][:, :width], columns, 0, 0).astype(jnp.bfloat16)
        new_moment, new_second, back = moments(turned, basis_left[s], factor, moment[s].T, second[s].T)
        moms.append(new_moment.T)
        secs.append(new_second.T)
        if line:
            near = send(back, MIDDLE)
            far = send(back, OVER)
            pair = send(back, INWARD)
            backs = jnp.concatenate([back, pair, near, far], axis=0)
            outer_step = dot(backs, turn[s][width : 2 * width], 0, 1).astype(jnp.bfloat16)
            handed = send(outer_step, OUTWARD)
            step = dot(backs, turn[s][:width], 0, 1).astype(jnp.bfloat16)
            step = jnp.where(end, handed, step)
        else:
            every = lax.all_gather(back, "blk")
            backs = jnp.concatenate([lax.dynamic_index_in_dim(every, i, 0, keepdims=False) for i in ids], axis=0)
            step = dot(backs, turn[s][:width], 0, 1).astype(jnp.bfloat16)
        step = step.reshape(owners, rows, width)
        returned = lax.all_to_all(step, "fsdp", split_axis=0, concat_axis=0, tiled=True)
        placed = placed.at[slots[:, s]].set(returned, unique_indices=True, mode="promise_in_bounds")

        own_rows = lax.dynamic_slice_in_dim(columns, place * width, width, 1)
        outer_left = dot(own_rows, columns, 0, 0)
        outer_right = jnp.concatenate(canonical([dot(own[s], g, 1, 1) for g in gathered[s]]), axis=1)
        weight = (1.0 - stat_decay) * (factor * factor)
        lefts.append((stat_decay * stat_left[s].T + weight * outer_left).T)
        rights.append((stat_decay * stat_right[s].T + weight * outer_right).T)

    return (placed, jnp.stack(lefts), jnp.stack(rights), jnp.stack(moms), jnp.stack(secs), grad_rms)


def solution(mesh):
    split = P("fsdp", None, "blk")
    whole = P("fsdp", None, None)
    return jax.shard_map(
        whole_step,
        mesh=mesh,
        in_specs=(P(None, "fsdp", "blk"), P(), split, split, whole, whole, split, split),
        out_specs=(P(None, "fsdp", "blk"), split, split, split, split, P()),
        check_vma=False,
    )
```

```python
import jax
import jax.numpy as jnp
from jax import lax
from jax.experimental import pallas as pl
from jax.experimental.pallas import tpu as pltpu
from jax.sharding import PartitionSpec as P


clip_level = 0.5
stat_decay = 0.95
beta_one = 0.9
beta_two = 0.95
epsilon = 1e-08


def dot(a, b, da, db):
    return lax.dot_general(a, b, (((da,), (db,)), ((), ())), preferred_element_type=jnp.float32)


def total_over(value, axes):
    for name in axes:
        size = lax.axis_size(name)
        if size & (size - 1):
            value = lax.psum(value, name)
            continue
        step = 1
        while step < size:
            value = value + lax.ppermute(value, name, [(i, i ^ step) for i in range(size)])
            step *= 2
    return value


def send(value, pairs):
    return lax.ppermute(value, "blk", pairs)


def take_kernel(slots, grad, send_ref, sum_ref):
    blocks, rows, width = grad.shape
    per = blocks // send_ref.shape[0]
    squares = jnp.zeros((rows, width), jnp.float32)
    for b in range(blocks):
        value = grad[b].astype(jnp.float32)
        squares += value * value
        send_ref[b // per, pl.ds(b % per * rows, rows), :] = grad[slots[b]]
    total = jnp.sum(jnp.sum(squares, axis=0, keepdims=True), axis=1, keepdims=True)
    sum_ref[...] = jnp.broadcast_to(total, sum_ref.shape)


def take(grad, owner_slots, owners):
    blocks, rows, width = grad.shape
    vmem = pl.BlockSpec(memory_space=pltpu.VMEM)
    return pl.pallas_call(
        take_kernel,
        out_shape=[
            jax.ShapeDtypeStruct((owners, blocks // owners * rows, width), grad.dtype),
            jax.ShapeDtypeStruct((owners, 128), jnp.float32),
        ],
        in_specs=[pl.BlockSpec(memory_space=pltpu.SMEM), vmem],
        out_specs=[vmem, vmem],
        name="take",
    )(owner_slots, grad)


def place_kernel(slots, returned, *rest):
    placed, sem = rest[-2:]
    copies = [pltpu.make_async_copy(returned.at[f], placed.at[slots[f]], sem.at[f]) for f in range(returned.shape[0])]
    for copy in copies:
        copy.start()
    for copy in copies:
        copy.wait()


def put(placed, shape, slots, returned):
    earlier = [] if placed is None else [placed]
    anywhere = pl.BlockSpec(memory_space=pl.ANY)
    return pl.pallas_call(
        place_kernel,
        out_shape=shape,
        in_specs=[pl.BlockSpec(memory_space=pltpu.SMEM), anywhere] + [anywhere] * len(earlier),
        out_specs=anywhere,
        scratch_shapes=[pltpu.SemaphoreType.DMA((returned.shape[0],))],
        input_output_aliases={2: 0} if earlier else {},
        compiler_params=pltpu.CompilerParams(vmem_limit_bytes=1 << 20),
        name="put",
    )(slots, returned, *earlier)


SWAP = [(0, 1), (1, 0), (2, 3), (3, 2)]
MIDDLE = [(1, 2), (2, 1)]
OVER = [(0, 2), (3, 1)]
INWARD = [(0, 1), (3, 2)]
OUTWARD = [(1, 0), (2, 3)]


def moments(turned, basis, factor, moment, second):
    rotated = factor * dot(turned, basis, 1, 0)
    new_moment = beta_one * moment + (1.0 - beta_one) * rotated
    new_second = beta_two * second + (1.0 - beta_two) * rotated * rotated
    scaled = (new_moment / (jnp.sqrt(new_second) + epsilon)).astype(jnp.bfloat16)
    back = dot(scaled, basis, 1, 1).astype(jnp.bfloat16)
    return new_moment, new_second, back


def whole_step(grad, owner_slots, stat_left, stat_right, basis_left, basis_right, moment, second):
    blocks, rows, width = grad.shape
    owners = lax.axis_size("fsdp")
    size = lax.axis_size("blk")
    per = blocks // owners
    order = rows * owners
    place = lax.axis_index("blk")
    line = size == 4
    slots = owner_slots.reshape(owners, per)

    upper = place >= 2
    end = (place == 0) | (place == 3)
    if line:
        near_at = jnp.where(upper, 1, 2)
        ids = [place, place ^ 1, near_at, jnp.where(upper, 0, 3)]
    else:
        ids = [lax.rem(place + k, size) for k in range(size)]

    def rearranged(matrix):
        matrix = jnp.concatenate([lax.dynamic_slice_in_dim(matrix, i * width, width, 0) for i in ids], axis=0)
        return jnp.concatenate([lax.dynamic_slice_in_dim(matrix, i * width, width, 1) for i in ids], axis=1)

    turn = []
    for s in range(per):
        turn.append(rearranged(basis_right[s]))

    own = []
    if line:
        sent, total = take(grad, owner_slots, owners)
        piece = lax.all_to_all(sent, "fsdp", split_axis=0, concat_axis=0, tiled=True)
        total = total_over(total, ("blk",))
        piece, total, *turn = lax.optimization_barrier((piece, total, *turn))
        total = lax.all_to_all(total, "fsdp", split_axis=0, concat_axis=0, tiled=True)
        total = jnp.sum(total[:, 0])
        for s in range(per):
            own.append(piece[:, s * rows : (s + 1) * rows, :width].reshape(order, width).T)
    else:
        for s in range(per):
            piece = grad.at[slots[:, s]].get(mode="promise_in_bounds", unique_indices=True)
            piece = lax.all_to_all(piece, "fsdp", split_axis=0, concat_axis=0, tiled=True)
            own.append(piece.reshape(order, width).T)

    if not line:
        total = total_over(jnp.sum(jnp.square(grad.astype(jnp.float32))).reshape(1, 1), ("fsdp", "blk"))[0, 0]
    grad_rms = jnp.sqrt(total / (blocks * order * order))
    factor = jnp.minimum(1.0, clip_level / grad_rms)

    def canonical(parts):
        if line:
            a, b, c, d = parts
            low = jnp.where(place == 0, a, b), jnp.where(place == 0, b, a)
            high = jnp.where(place == 2, a, b), jnp.where(place == 2, b, a)
            return [
                jnp.where(upper, d, low[0]),
                jnp.where(upper, c, low[1]),
                jnp.where(upper, high[0], c),
                jnp.where(upper, high[1], d),
            ]
        return [sum(jnp.where(i == k, p, 0) for i, p in zip(ids, parts)) for k in range(len(parts))]

    gathered = []
    if line:
        pairs = send(jnp.stack(own), SWAP)
        for s in range(per):
            pair = pairs[s]
            near = send(own[s], MIDDLE)
            far = send(own[s], OVER)
            passed = send(jnp.stack([near, far]), OUTWARD)
            near, far = jnp.where(end, passed[0], near), jnp.where(end, passed[1], far)
            gathered.append([own[s], pair, near, far])
    else:
        for s in range(per):
            every = lax.all_gather(own[s], "blk")
            gathered.append([lax.dynamic_index_in_dim(every, i, 0, keepdims=False) for i in ids])

    lefts, rights, moms, secs = [], [], [], []
    placed = None if line else jnp.zeros_like(grad)
    for s in range(per):
        columns = jnp.concatenate(gathered[s], axis=0)
        turned = dot(turn[s][:, :width], columns, 0, 0).astype(jnp.bfloat16)
        new_moment, new_second, back = moments(turned, basis_left[s], factor, moment[s].T, second[s].T)
        moms.append(new_moment.T)
        secs.append(new_second.T)
        if line:
            near = send(back, MIDDLE)
            far = send(back, OVER)
            pair = send(back, INWARD)
            backs = jnp.concatenate([back, pair, near, far], axis=0)
            outer_step = dot(backs, turn[s][width : 2 * width], 0, 1).astype(jnp.bfloat16)
            handed = send(outer_step, OUTWARD)
            step = dot(backs, turn[s][:width], 0, 1).astype(jnp.bfloat16)
            step = jnp.where(end, handed, step)
        else:
            every = lax.all_gather(back, "blk")
            backs = jnp.concatenate([lax.dynamic_index_in_dim(every, i, 0, keepdims=False) for i in ids], axis=0)
            step = dot(backs, turn[s][:width], 0, 1).astype(jnp.bfloat16)
        step = step.reshape(owners, rows, width)
        returned = lax.all_to_all(step, "fsdp", split_axis=0, concat_axis=0, tiled=True)
        if line:
            placed = put(placed, jax.ShapeDtypeStruct(grad.shape, grad.dtype), slots[:, s], returned)
        else:
            placed = placed.at[slots[:, s]].set(returned, unique_indices=True, mode="promise_in_bounds")

        own_rows = lax.dynamic_slice_in_dim(columns, place * width, width, 1)
        outer_left = dot(own_rows, columns, 0, 0)
        outer_right = jnp.concatenate(canonical([dot(own[s], g, 1, 1) for g in gathered[s]]), axis=1)
        weight = (1.0 - stat_decay) * (factor * factor)
        lefts.append((stat_decay * stat_left[s].T + weight * outer_left).T)
        rights.append((stat_decay * stat_right[s].T + weight * outer_right).T)

    return (placed, jnp.stack(lefts), jnp.stack(rights), jnp.stack(moms), jnp.stack(secs), grad_rms)


def solution(mesh):
    split = P("fsdp", None, "blk")
    whole = P("fsdp", None, None)
    return jax.shard_map(
        whole_step,
        mesh=mesh,
        in_specs=(P(None, "fsdp", "blk"), P(), split, split, whole, whole, split, split),
        out_specs=(P(None, "fsdp", "blk"), split, split, split, split, P()),
        check_vma=False,
    )
```

```python
import jax
import jax.numpy as jnp
from jax import lax
from jax.experimental import pallas as pl
from jax.experimental.pallas import tpu as pltpu
from jax.sharding import PartitionSpec as P


clip_level = 0.5
stat_decay = 0.95
beta_one = 0.9
beta_two = 0.95
epsilon = 1e-08


def dot(a, b, da, db):
    return lax.dot_general(a, b, (((da,), (db,)), ((), ())), preferred_element_type=jnp.float32)


def total_over(value, axes):
    for name in axes:
        size = lax.axis_size(name)
        if size & (size - 1):
            value = lax.psum(value, name)
            continue
        step = 1
        while step < size:
            value = value + lax.ppermute(value, name, [(i, i ^ step) for i in range(size)])
            step *= 2
    return value


def send(value, pairs):
    return lax.ppermute(value, "blk", pairs)


def take_kernel(slots, grad, send_ref, sum_ref):
    blocks, rows, width = grad.shape
    per = blocks // send_ref.shape[0]
    squares = jnp.zeros((rows, width), jnp.float32)
    for b in range(blocks):
        value = grad[b].astype(jnp.float32)
        squares += value * value
        send_ref[b // per, pl.ds(b % per * rows, rows), :] = grad[slots[b]]
    total = jnp.sum(jnp.sum(squares, axis=0, keepdims=True), axis=1, keepdims=True)
    sum_ref[...] = jnp.broadcast_to(total, sum_ref.shape)


def take(grad, owner_slots, owners):
    blocks, rows, width = grad.shape
    vmem = pl.BlockSpec(memory_space=pltpu.VMEM)
    return pl.pallas_call(
        take_kernel,
        out_shape=[
            jax.ShapeDtypeStruct((owners, blocks // owners * rows, width), grad.dtype),
            jax.ShapeDtypeStruct((owners, 128), jnp.float32),
        ],
        in_specs=[pl.BlockSpec(memory_space=pltpu.SMEM), vmem],
        out_specs=[vmem, vmem],
        name="take",
    )(owner_slots, grad)


def place_kernel(slots, returned, *rest):
    placed, sem = rest[-2:]
    copies = [pltpu.make_async_copy(returned.at[f], placed.at[slots[f]], sem.at[f]) for f in range(returned.shape[0])]
    for copy in copies:
        copy.start()
    for copy in copies:
        copy.wait()


def put(placed, shape, slots, returned):
    earlier = [] if placed is None else [placed]
    anywhere = pl.BlockSpec(memory_space=pl.ANY)
    return pl.pallas_call(
        place_kernel,
        out_shape=shape,
        in_specs=[pl.BlockSpec(memory_space=pltpu.SMEM), anywhere] + [anywhere] * len(earlier),
        out_specs=anywhere,
        scratch_shapes=[pltpu.SemaphoreType.DMA((returned.shape[0],))],
        input_output_aliases={2: 0} if earlier else {},
        compiler_params=pltpu.CompilerParams(vmem_limit_bytes=1 << 20),
        name="put",
    )(slots, returned, *earlier)


def at_block(index, width):
    return pl.ds(pl.multiple_of(index * width, width), width)


def turn_kernel(ids, own, pair, near, far, passed_near, passed_far, columns, basis, rotated, whole):
    width = own.shape[0]
    whole[at_block(ids[0], width), :] = own[...]
    whole[at_block(ids[1], width), :] = pair[...]
    whole[at_block(ids[2], width), :] = near[...] + passed_near[...]
    whole[at_block(ids[3], width), :] = far[...] + passed_far[...]
    turned = dot(columns[...], whole[...], 0, 0)
    rotated[...] = dot(turned.astype(jnp.bfloat16), basis[...], 1, 0)


def turn_own(ids, blocks, columns, basis):
    vmem = pl.BlockSpec(memory_space=pltpu.VMEM)
    return pl.pallas_call(
        turn_kernel,
        out_shape=[
            jax.ShapeDtypeStruct(blocks[0].shape, jnp.float32),
            jax.ShapeDtypeStruct(basis.shape, blocks[0].dtype),
        ],
        in_specs=[pl.BlockSpec(memory_space=pltpu.SMEM)] + [vmem] * 8,
        out_specs=[vmem, vmem],
        name="turn_own",
    )(ids, *blocks, columns, basis)


def update_kernel(ids, back, pair, near, far, basis, step, handed, whole):
    width = back.shape[0]

    @pl.when((ids[0] == 1) | (ids[0] == 2))
    def _():
        for c, block in enumerate((back, pair, near, far)):
            whole[at_block(ids[c], width), :] = block[...]
        handed[...] = dot(basis[at_block(ids[1], width), :], whole[...], 1, 0).astype(handed.dtype)
        step[...] = dot(basis[at_block(ids[0], width), :], whole[...], 1, 0).astype(step.dtype)


def update_both(ids, blocks, basis):
    shape = jax.ShapeDtypeStruct(blocks[0].shape, blocks[0].dtype)
    vmem = pl.BlockSpec(memory_space=pltpu.VMEM)
    return pl.pallas_call(
        update_kernel,
        out_shape=[shape, shape],
        in_specs=[pl.BlockSpec(memory_space=pltpu.SMEM)] + [vmem] * 5,
        out_specs=[vmem, vmem],
        scratch_shapes=[pltpu.VMEM(basis.shape, blocks[0].dtype)],
        name="update_both",
    )(ids, *blocks, basis)


SWAP = [(0, 1), (1, 0), (2, 3), (3, 2)]
MIDDLE = [(1, 2), (2, 1)]
OVER = [(0, 2), (3, 1)]
INWARD = [(0, 1), (3, 2)]
OUTWARD = [(1, 0), (2, 3)]


def moments(rotated, basis, factor, moment, second):
    rotated = factor * rotated
    new_moment = beta_one * moment + (1.0 - beta_one) * rotated
    new_second = beta_two * second + (1.0 - beta_two) * rotated * rotated
    scaled = (new_moment / (jnp.sqrt(new_second) + epsilon)).astype(jnp.bfloat16)
    back = dot(scaled, basis, 1, 1).astype(jnp.bfloat16)
    return new_moment, new_second, back


def whole_step(grad, owner_slots, stat_left, stat_right, basis_left, basis_right, moment, second):
    blocks, rows, width = grad.shape
    owners = lax.axis_size("fsdp")
    size = lax.axis_size("blk")
    per = blocks // owners
    order = rows * owners
    place = lax.axis_index("blk")
    line = size == 4
    slots = owner_slots.reshape(owners, per)

    upper = place >= 2
    end = (place == 0) | (place == 3)
    if line:
        near_at = jnp.where(upper, 1, 2)
        ids = [place, place ^ 1, near_at, jnp.where(upper, 0, 3)]
        order_ids = jnp.stack(ids).astype(jnp.int32)

    turn = []
    for s in range(per):
        turn.append(lax.dynamic_slice_in_dim(basis_right[s], place * width, width, 1))
    own = []
    if line:
        sent, total = take(grad, owner_slots, owners)
        piece = lax.all_to_all(sent, "fsdp", split_axis=0, concat_axis=0, tiled=True)
        total = total_over(total, ("blk",))
        piece, total, turn, order_ids = lax.optimization_barrier((piece, total, turn, order_ids))
        total = lax.all_to_all(total, "fsdp", split_axis=0, concat_axis=0, tiled=True)
        total = jnp.sum(total[:, 0])
        for s in range(per):
            own.append(piece[:, s * rows : (s + 1) * rows, :width].reshape(order, width).T)
    else:
        for s in range(per):
            piece = grad.at[slots[:, s]].get(mode="promise_in_bounds", unique_indices=True)
            piece = lax.all_to_all(piece, "fsdp", split_axis=0, concat_axis=0, tiled=True)
            own.append(piece.reshape(order, width).T)

    if not line:
        total = total_over(jnp.sum(jnp.square(grad.astype(jnp.float32))).reshape(1, 1), ("fsdp", "blk"))[0, 0]
    grad_rms = jnp.sqrt(total / (blocks * order * order))
    factor = jnp.minimum(1.0, clip_level / grad_rms)

    own = own[:1] + [lax.optimization_barrier(block) for block in own[1:]]

    gathered, rotations = [], []
    for s in range(per):
        if line:
            near = send(own[s], MIDDLE)
            pair = send(own[s], SWAP)
            far = send(own[s], OVER)
            passed_near = send(near, OUTWARD)
            passed_far = send(far, OUTWARD)
            blocks_now = [own[s], pair, near, far, passed_near, passed_far]
            rotated, columns = turn_own(order_ids, blocks_now, turn[s], basis_left[s])
        else:
            columns = lax.all_gather(own[s], "blk", axis=0, tiled=True)
            rotated = dot(dot(turn[s], columns, 0, 0).astype(jnp.bfloat16), basis_left[s], 1, 0)
        gathered.append(columns)
        rotations.append(rotated)

    lefts, rights, moms, secs = [], [], [], []
    placed = None if line else jnp.zeros_like(grad)
    for s in range(per):
        new_moment, new_second, back = moments(rotations[s], basis_left[s], factor, moment[s].T, second[s].T)
        moms.append(new_moment.T)
        secs.append(new_second.T)
        if line:
            near = send(back, MIDDLE)
            far = send(back, OVER)
            pair = send(back, INWARD)
            step, handed = update_both(order_ids, [back, pair, near, far], basis_right[s])
            handed = send(handed, OUTWARD)
            step = jnp.where(end, handed, step).T
        else:
            backs = lax.all_gather(back, "blk", axis=0, tiled=True)
            right_rows = lax.dynamic_slice_in_dim(basis_right[s], place * width, width, 0)
            step = dot(backs, right_rows, 0, 1).astype(jnp.bfloat16)
        step = step.reshape(owners, rows, width)
        returned = lax.all_to_all(step, "fsdp", split_axis=0, concat_axis=0, tiled=True)
        if line:
            placed = put(placed, jax.ShapeDtypeStruct(grad.shape, grad.dtype), slots[:, s], returned)
        else:
            placed = placed.at[slots[:, s]].set(returned, unique_indices=True, mode="promise_in_bounds")

        columns = gathered[s]
        own_rows = lax.dynamic_slice_in_dim(columns, place * width, width, 1)
        outer_left = dot(own_rows, columns, 0, 0)
        outer_right = dot(own[s], columns, 1, 1)
        weight = (1.0 - stat_decay) * (factor * factor)
        lefts.append((stat_decay * stat_left[s].T + weight * outer_left).T)
        rights.append((stat_decay * stat_right[s].T + weight * outer_right).T)

    stacked = [jnp.stack(parts) for parts in (lefts, rights)]
    stacked += [jnp.stack(parts) for parts in (moms, secs)]
    return (placed, *stacked, grad_rms)


def solution(mesh):
    split = P("fsdp", None, "blk")
    whole = P("fsdp", None, None)
    return jax.shard_map(
        whole_step,
        mesh=mesh,
        in_specs=(P(None, "fsdp", "blk"), P(), split, split, whole, whole, split, split),
        out_specs=(P(None, "fsdp", "blk"), split, split, split, split, P()),
        check_vma=False,
    )
```

```python
import functools

import jax
import jax.numpy as jnp
from jax import lax
from jax.experimental import pallas as pl
from jax.experimental.pallas import tpu as pltpu
from jax.sharding import PartitionSpec as P


clip_level = 0.5
stat_decay = 0.95
beta_one = 0.9
beta_two = 0.95
epsilon = 1e-08


def dot(a, b, da, db):
    return lax.dot_general(a, b, (((da,), (db,)), ((), ())), preferred_element_type=jnp.float32)


def total_over(value, axes):
    for name in axes:
        size = lax.axis_size(name)
        if size & (size - 1):
            value = lax.psum(value, name)
            continue
        step = 1
        while step < size:
            value = value + lax.ppermute(value, name, [(i, i ^ step) for i in range(size)])
            step *= 2
    return value


def send(value, pairs):
    return lax.ppermute(value, "blk", pairs)


def take_kernel(slots, grad, send_ref, sum_ref):
    blocks, rows, width = grad.shape
    per = blocks // send_ref.shape[0]
    squares = jnp.zeros((rows, width), jnp.float32)
    for b in range(blocks):
        value = grad[b].astype(jnp.float32)
        squares += value * value
        send_ref[b // per, pl.ds(b % per * rows, rows), :] = grad[slots[b]]
    total = jnp.sum(jnp.sum(squares, axis=0, keepdims=True), axis=1, keepdims=True)
    sum_ref[...] = jnp.broadcast_to(total, sum_ref.shape)


def take(grad, owner_slots, owners):
    blocks, rows, width = grad.shape
    vmem = pl.BlockSpec(memory_space=pltpu.VMEM)
    return pl.pallas_call(
        take_kernel,
        out_shape=[
            jax.ShapeDtypeStruct((owners, blocks // owners * rows, width), grad.dtype),
            jax.ShapeDtypeStruct((owners, 128), jnp.float32),
        ],
        in_specs=[pl.BlockSpec(memory_space=pltpu.SMEM), vmem],
        out_specs=[vmem, vmem],
        name="take",
    )(owner_slots, grad)


def place_kernel(slots, returned, *rest):
    placed, sem = rest[-2:]
    copies = [pltpu.make_async_copy(returned.at[f], placed.at[slots[f]], sem.at[f]) for f in range(returned.shape[0])]
    for copy in copies:
        copy.start()
    for copy in copies:
        copy.wait()


def put(placed, shape, slots, returned):
    earlier = [] if placed is None else [placed]
    anywhere = pl.BlockSpec(memory_space=pl.ANY)
    return pl.pallas_call(
        place_kernel,
        out_shape=shape,
        in_specs=[pl.BlockSpec(memory_space=pltpu.SMEM), anywhere] + [anywhere] * len(earlier),
        out_specs=anywhere,
        scratch_shapes=[pltpu.SemaphoreType.DMA((returned.shape[0],))],
        input_output_aliases={2: 0} if earlier else {},
        compiler_params=pltpu.CompilerParams(vmem_limit_bytes=1 << 20),
        name="put",
    )(slots, returned, *earlier)


def at_block(index, width):
    return pl.ds(pl.multiple_of(index * width, width), width)


def turn_kernel(ids, own, pair, near, far, passed_near, passed_far, columns, basis, rotated, whole):
    width = own.shape[0]
    whole[at_block(ids[0], width), :] = own[...]
    whole[at_block(ids[1], width), :] = pair[...]
    whole[at_block(ids[2], width), :] = near[...] + passed_near[...]
    whole[at_block(ids[3], width), :] = far[...] + passed_far[...]
    turned = dot(columns[...], whole[...], 0, 0)
    rotated[...] = dot(turned.astype(jnp.bfloat16), basis[...], 1, 0)


def turn_own(ids, blocks, columns, basis):
    vmem = pl.BlockSpec(memory_space=pltpu.VMEM)
    return pl.pallas_call(
        turn_kernel,
        out_shape=[
            jax.ShapeDtypeStruct(blocks[0].shape, jnp.float32),
            jax.ShapeDtypeStruct(basis.shape, blocks[0].dtype),
        ],
        in_specs=[pl.BlockSpec(memory_space=pltpu.SMEM)] + [vmem] * 8,
        out_specs=[vmem, vmem],
        name="turn_own",
    )(ids, *blocks, columns, basis)


def update_kernel(which, ids, back, pair, near, far, basis, step, whole):
    width = back.shape[0]

    @pl.when((ids[0] == 1) | (ids[0] == 2))
    def _():
        for c, block in enumerate((back, pair, near, far)):
            whole[at_block(ids[c], width), :] = block[...]
        step[...] = dot(basis[at_block(ids[which], width), :], whole[...], 1, 0).astype(step.dtype)


def update(which, ids, blocks, basis):
    vmem = pl.BlockSpec(memory_space=pltpu.VMEM)
    return pl.pallas_call(
        functools.partial(update_kernel, which),
        out_shape=jax.ShapeDtypeStruct(blocks[0].shape, blocks[0].dtype),
        in_specs=[pl.BlockSpec(memory_space=pltpu.SMEM)] + [vmem] * 5,
        out_specs=vmem,
        scratch_shapes=[pltpu.VMEM(basis.shape, blocks[0].dtype)],
        name="update_pair" if which else "update_own",
    )(ids, *blocks, basis)


def both_kernel(ids, back, pair, near, far, basis, step, handed, whole):
    width = back.shape[0]

    @pl.when((ids[0] == 1) | (ids[0] == 2))
    def _():
        for c, block in enumerate((back, pair, near, far)):
            whole[at_block(ids[c], width), :] = block[...]
        handed[...] = dot(basis[at_block(ids[1], width), :], whole[...], 1, 0).astype(handed.dtype)
        step[...] = dot(basis[at_block(ids[0], width), :], whole[...], 1, 0).astype(step.dtype)


def update_both(ids, blocks, basis):
    shape = jax.ShapeDtypeStruct(blocks[0].shape, blocks[0].dtype)
    vmem = pl.BlockSpec(memory_space=pltpu.VMEM)
    return pl.pallas_call(
        both_kernel,
        out_shape=[shape, shape],
        in_specs=[pl.BlockSpec(memory_space=pltpu.SMEM)] + [vmem] * 5,
        out_specs=[vmem, vmem],
        scratch_shapes=[pltpu.VMEM(basis.shape, blocks[0].dtype)],
        name="update_both",
    )(ids, *blocks, basis)


SWAP = [(0, 1), (1, 0), (2, 3), (3, 2)]
MIDDLE = [(1, 2), (2, 1)]
OVER = [(0, 2), (3, 1)]
INWARD = [(0, 1), (3, 2)]
OUTWARD = [(1, 0), (2, 3)]


def moments(rotated, basis, factor, moment, second):
    rotated = factor * rotated
    new_moment = beta_one * moment + (1.0 - beta_one) * rotated
    new_second = beta_two * second + (1.0 - beta_two) * rotated * rotated
    scaled = (new_moment / (jnp.sqrt(new_second) + epsilon)).astype(jnp.bfloat16)
    back = dot(scaled, basis, 1, 1).astype(jnp.bfloat16)
    return new_moment, new_second, back


def whole_step(grad, owner_slots, stat_left, stat_right, basis_left, basis_right, moment, second):
    blocks, rows, width = grad.shape
    owners = lax.axis_size("fsdp")
    size = lax.axis_size("blk")
    per = blocks // owners
    order = rows * owners
    place = lax.axis_index("blk")
    line = size == 4
    slots = owner_slots.reshape(owners, per)

    upper = place >= 2
    end = (place == 0) | (place == 3)
    if line:
        near_at = jnp.where(upper, 1, 2)
        ids = [place, place ^ 1, near_at, jnp.where(upper, 0, 3)]
        order_ids = jnp.stack(ids).astype(jnp.int32)

    turn = []
    for s in range(per):
        turn.append(lax.dynamic_slice_in_dim(basis_right[s], place * width, width, 1))
    own = []
    if line:
        sent, total = take(grad, owner_slots, owners)
        piece = lax.all_to_all(sent, "fsdp", split_axis=0, concat_axis=0, tiled=True)
        total = total_over(total, ("blk",))
        piece, total, turn, order_ids = lax.optimization_barrier((piece, total, turn, order_ids))
        total = lax.all_to_all(total, "fsdp", split_axis=0, concat_axis=0, tiled=True)
        total = jnp.sum(total[:, 0])
        for s in range(per):
            own.append(piece[:, s * rows : (s + 1) * rows, :width].reshape(order, width).T)
    else:
        for s in range(per):
            piece = grad.at[slots[:, s]].get(mode="promise_in_bounds", unique_indices=True)
            piece = lax.all_to_all(piece, "fsdp", split_axis=0, concat_axis=0, tiled=True)
            own.append(piece.reshape(order, width).T)

    if not line:
        total = total_over(jnp.sum(jnp.square(grad.astype(jnp.float32))).reshape(1, 1), ("fsdp", "blk"))[0, 0]
    grad_rms = jnp.sqrt(total / (blocks * order * order))
    factor = jnp.minimum(1.0, clip_level / grad_rms)

    own = own[:1] + [lax.optimization_barrier(block) for block in own[1:]]

    gathered, rotations = [], []
    for s in range(per):
        if line:
            near = send(own[s], MIDDLE)
            pair = send(own[s], SWAP)
            far = send(own[s], OVER)
            passed_near = send(near, OUTWARD)
            passed_far = send(far, OUTWARD)
            blocks_now = [own[s], pair, near, far, passed_near, passed_far]
            rotated, columns = turn_own(order_ids, blocks_now, turn[s], basis_left[s])
        else:
            columns = lax.all_gather(own[s], "blk", axis=0, tiled=True)
            rotated = dot(dot(turn[s], columns, 0, 0).astype(jnp.bfloat16), basis_left[s], 1, 0)
        gathered.append(columns)
        rotations.append(rotated)

    lefts, rights, moms, secs = [], [], [], []
    placed = None if line else jnp.zeros_like(grad)
    for s in range(per):
        new_moment, new_second, back = moments(rotations[s], basis_left[s], factor, moment[s].T, second[s].T)
        moms.append(new_moment.T)
        secs.append(new_second.T)
        if line:
            near = send(back, MIDDLE)
            far = send(back, OVER)
            pair = send(back, INWARD)
            if s + 1 < per:
                step, handed = update_both(order_ids, [back, pair, near, far], basis_right[s])
            else:
                handed = update(1, order_ids, [back, pair, near, far], basis_right[s])
            if s + 1 == per:
                step = update(0, order_ids, [back, pair, near, far], basis_right[s])
            handed = send(handed, OUTWARD)
            step = jnp.where(end, handed, step).T
        else:
            backs = lax.all_gather(back, "blk", axis=0, tiled=True)
            right_rows = lax.dynamic_slice_in_dim(basis_right[s], place * width, width, 0)
            step = dot(backs, right_rows, 0, 1).astype(jnp.bfloat16)
        step = step.reshape(owners, rows, width)
        returned = lax.all_to_all(step, "fsdp", split_axis=0, concat_axis=0, tiled=True)
        if line:
            placed = put(placed, jax.ShapeDtypeStruct(grad.shape, grad.dtype), slots[:, s], returned)
        else:
            placed = placed.at[slots[:, s]].set(returned, unique_indices=True, mode="promise_in_bounds")

        columns = gathered[s]
        own_rows = lax.dynamic_slice_in_dim(columns, place * width, width, 1)
        outer_left = dot(own_rows, columns, 0, 0)
        outer_right = dot(own[s], columns, 1, 1)
        weight = (1.0 - stat_decay) * (factor * factor)
        lefts.append((stat_decay * stat_left[s].T + weight * outer_left).T)
        rights.append((stat_decay * stat_right[s].T + weight * outer_right).T)

    stacked = [jnp.stack(parts) for parts in (lefts, rights)]
    stacked += [jnp.stack(parts) for parts in (moms, secs)]
    return (placed, *stacked, grad_rms)


def solution(mesh):
    split = P("fsdp", None, "blk")
    whole = P("fsdp", None, None)
    return jax.shard_map(
        whole_step,
        mesh=mesh,
        in_specs=(P(None, "fsdp", "blk"), P(), split, split, whole, whole, split, split),
        out_specs=(P(None, "fsdp", "blk"), split, split, split, split, P()),
        check_vma=False,
    )
```
